32 devices in a mesh: dp: 4 (over z), ctx: 8 (over y, x, core).
Axes of the slice: x: 2, y: 2, z: 4, core: 2. Of those that a mesh axis runs over, the one named last changes fastest.
Arguments:
- hidden_in: bfloat16 [2, 1024, 4, 576], P(None, 'ctx', 'dp'), may hold values from -6 to 6
- piece_starts: int32 [2, 4, 1], P(None, 'dp'), may hold values from 0 to 768, as said below
- out_grad: bfloat16 [2, 1024, 4, 576], P(None, 'ctx', 'dp'), may hold values from -6 to 6
- attn_gain: bfloat16 [576], P('ctx'), may hold values from 0.25 to 1.75
- w_query: bfloat16 [576, 576], P('ctx'), may hold values from -0.25 to 0.25
- w_key: bfloat16 [576, 192], P('ctx'), may hold values from -0.25 to 0.25
- w_value: bfloat16 [576, 192], P('ctx'), may hold values from -0.25 to 0.25
- w_out: bfloat16 [576, 576], P('ctx'), may hold values from -1 to 1
- mlp_gain: bfloat16 [576], P('ctx'), may hold values from 0.25 to 1.75
- w_gate: bfloat16 [576, 1536], P('ctx'), may hold values from -0.25 to 0.25
- w_up: bfloat16 [576, 1536], P('ctx'), may hold values from -0.25 to 0.25
- w_down: bfloat16 [1536, 576], P('ctx'), may hold values from -0.15625 to 0.15625
Outputs:
- hidden_out: bfloat16 [2, 1024, 4, 576], P(None, 'ctx', 'dp')
- in_grad: float32 [2, 1024, 4, 576], P(None, 'ctx', 'dp')
- attn_gain_grad: float32 [576], P('ctx')
- w_query_grad: float32 [576, 576], P('ctx')
- w_key_grad: float32 [576, 192], P('ctx')
- w_value_grad: float32 [576, 192], P('ctx')
- w_out_grad: float32 [576, 576], P('ctx')
- mlp_gain_grad: float32 [576], P('ctx')
- w_gate_grad: float32 [576, 1536], P('ctx')
- w_up_grad: float32 [576, 1536], P('ctx')
- w_down_grad: float32 [1536, 576], P('ctx')
The draws below stay inside these ranges and needn't reach their ends.
Inputs may be any that keep to these rules, and one draw needn't show every extreme that they name: `piece_starts`: each sequence holds 1 picture pieces of 256 positions in rising order, each wholly inside the sequence, no two intersecting.
All inputs are finite; a program needn't handle non-finite values.
Results may differ from the reference program's by a relative error of at most 0.02.
Values may be sent and summed in bfloat16 or wider, within the bound.
No kernel may reach another device: no remote copies, remote signals or barrier semaphores. Data moves between devices by JAX's collectives and lax.ppermute only.
A program may use at most 128 MiB of HBM per device.

```python
import math
import jax
import jax.numpy as jnp
from jax import lax

D = 576
HQ = 9
KVH = 3
HD = 64
FF = 1536
MICRO = 2
PIECE = 256
LENGTH = 1024
SEQS_MB = 4
NPIECE = 1


def draw_piece_starts(key, part):
    slot_len = LENGTH // NPIECE
    spare_len = slot_len - PIECE + 1
    offsets = jax.random.randint(key, (MICRO, SEQS_MB, NPIECE), 0, spare_len, dtype=jnp.int32)
    offsets = offsets.at[0, 0, 0].set(0)
    offsets = offsets.at[MICRO - 1, SEQS_MB - 1, NPIECE - 1].set(spare_len - 1)
    return (offsets + jnp.arange(NPIECE, dtype=jnp.int32)[None, None, :] * slot_len).astype(jnp.int32)


def level_of(key, dims, pieces, smallest, high):
    factor_of, own = 1.0, jax.random.fold_in(key, 6)
    for position, shards_of in pieces:
        heights = jnp.exp(jax.random.uniform(jax.random.fold_in(own, position), (shards_of,), jnp.float32, smallest / len(pieces), high / len(pieces)))
        factor_of = factor_of * jnp.repeat(heights, dims[position] // shards_of).reshape([-1 if axis == position else 1 for axis in range(len(dims))])
    return factor_of


def gaussian(key, shape, deviation, reach, cuts=(), kind=jnp.bfloat16):
    entries = jax.random.normal(key, shape, jnp.float32) * deviation
    if len(cuts) > 0:
        entries = level_of(key, shape, cuts, -0.22, 0.18) * entries
    return jnp.clip(entries, min=-reach, max=reach).astype(kind)


def setup_inputs(seed: int = 0) -> dict:
    keys = jax.random.split(jax.random.key(seed), 13)
    return {
        "hidden_in": gaussian(keys[0], (MICRO, LENGTH, SEQS_MB, D), 1.0, 6.0, ((1, 8), (2, 4))),
        "piece_starts": draw_piece_starts(jax.random.fold_in(keys[12], 71), 0),
        "out_grad": gaussian(keys[2], (MICRO, LENGTH, SEQS_MB, D), 1.0, 6.0, ((1, 8), (2, 4))),
        "attn_gain": jnp.clip(1.0 + 0.15 * jax.random.normal(keys[3], (D,), jnp.float32), 0.25, 1.75).astype(jnp.bfloat16),
        "w_query": gaussian(keys[4], (D, HQ * HD), D ** -0.5, 0.25, ((0, 8),)),
        "w_key": gaussian(keys[5], (D, KVH * HD), D ** -0.5, 0.25, ((0, 8),)),
        "w_value": gaussian(keys[6], (D, KVH * HD), D ** -0.5, 0.25, ((0, 8),)),
        "w_out": gaussian(keys[7], (HQ * HD, D), (max(D * 64 // LENGTH, 8)) ** -0.5, 1.0, ((0, 8),)),
        "mlp_gain": jnp.clip(1.0 + 0.15 * jax.random.normal(keys[8], (D,), jnp.float32), 0.25, 1.75).astype(jnp.bfloat16),
        "w_gate": gaussian(keys[9], (D, FF), D ** -0.5, 0.25, ((0, 8),)),
        "w_up": gaussian(keys[10], (D, FF), D ** -0.5, 0.25, ((0, 8),)),
        "w_down": gaussian(keys[11], (FF, D), FF ** -0.5, 0.15625, ((0, 8),)),
    }


EPS = 1e-05
MASKED = -1e+30
HIGH = lax.Precision.HIGHEST

@jax.custom_vjp
def low(v):
    return lax.optimization_barrier(v.astype(jnp.bfloat16)).astype(jnp.float32)

@jax.custom_vjp
def low_back(v):
    return v

def low_keep(v):
    return (low(v), None)

def low_pass(kept, grad):
    return (grad,)

def back_keep(v):
    return (v, None)

def back_low(kept, grad):
    return (low(grad),)
low.defvjp(low_keep, low_pass)
low_back.defvjp(back_keep, back_low)

def product(left, right):
    return jnp.dot(left, right, precision=HIGH, preferred_element_type=jnp.float32)

def rope_tables(positions):
    halfway = HD // 2
    frequency = 10000.0 ** (-jnp.arange(halfway, dtype=jnp.float32) / halfway)
    angles = positions.astype(jnp.float32)[:, None] * frequency[None, :]
    return (jnp.cos(angles), jnp.sin(angles))

def rotate(values, cosine, sine_tab):
    halfway = values.shape[-1] // 2
    former = values[..., :halfway]
    latter = values[..., halfway:]
    cosine = cosine[:, None, :]
    sine_tab = sine_tab[:, None, :]
    return jnp.concatenate([former * cosine - latter * sine_tab, latter * cosine + former * sine_tab], axis=-1)

def piece_index(positions, starts):
    inside = (positions[:, None] >= starts[None, :]) & (positions[:, None] < starts[None, :] + PIECE)
    numbers = jnp.arange(1, NPIECE + 1, dtype=jnp.int32)
    return lax.optimization_barrier(jnp.sum(jnp.where(inside, numbers[None, :], 0), axis=1)).astype(jnp.int32) - 1

def layer(sequence, starts, attn_gain, w_query, w_key, w_value, w_out, mlp_gain, w_gate, w_up, w_down):
    groups = HQ // KVH
    positions = jnp.arange(LENGTH, dtype=jnp.int32)
    cosine, sine_tab = rope_tables(positions)
    labels = piece_index(positions, starts)
    scale_one = lax.rsqrt(lax.optimization_barrier(jnp.mean(sequence * sequence, axis=1, keepdims=True)) + EPS)
    normed = low(sequence * scale_one * attn_gain)
    queries = product(normed, w_query).reshape(LENGTH, HQ, HD)
    key_rows = product(normed, w_key).reshape(LENGTH, KVH, HD)
    values = low(low_back(product(normed, w_value))).reshape(LENGTH, KVH, HD)
    queries = low(rotate(low_back(queries), cosine, sine_tab))
    key_rows = low(rotate(low_back(key_rows), cosine, sine_tab))
    query_span = math.gcd(LENGTH, 128)
    blocks = LENGTH // query_span
    query_blocks = queries.reshape(blocks, query_span, KVH, groups, HD)
    pos_blocks = positions.reshape(blocks, query_span)
    label_blocks = labels.reshape(blocks, query_span)

    def attend(inputs_now):
        block_query, block_pos, block_labels = inputs_now
        scores = jnp.einsum('qngd,knd->ngqk', block_query, key_rows, precision=HIGH, preferred_element_type=jnp.float32)
        scores = low_back(scores * 0.125)
        allowed = (positions[None, :] <= block_pos[:, None]) | (block_labels[:, None] == labels[None, :]) & (block_labels[:, None] >= 0)
        masked = jnp.where(allowed[None, None], scores, MASKED)
        highest = lax.optimization_barrier(jnp.max(masked, axis=-1, keepdims=True))
        expo = jnp.exp(masked - highest)
        weights = low(expo / lax.optimization_barrier(jnp.sum(expo, axis=-1, keepdims=True)))
        mixed_out = jnp.einsum('ngqk,knd->qngd', weights, values, precision=HIGH, preferred_element_type=jnp.float32)
        return mixed_out.reshape(query_span, HQ * HD)
    attended = lax.map(jax.checkpoint(attend), (query_blocks, pos_blocks, label_blocks))
    attended = low(low_back(attended.reshape(LENGTH, HQ * HD)))
    middle = sequence + low_back(product(attended, w_out))
    scale_two = lax.rsqrt(lax.optimization_barrier(jnp.mean(middle * middle, axis=1, keepdims=True)) + EPS)
    normed_two = low(middle * scale_two * mlp_gain)
    gate_pre = low_back(product(normed_two, w_gate))
    upward = low_back(product(normed_two, w_up))
    hidden = low(gate_pre * jax.nn.sigmoid(gate_pre) * upward)
    return middle + product(hidden, w_down)

def reference(hidden_in, piece_starts, out_grad, attn_gain, w_query, w_key, w_value, w_out, mlp_gain, w_gate, w_up, w_down):
    params = tuple((member.astype(jnp.float32) for member in (attn_gain, w_query, w_key, w_value, w_out, mlp_gain, w_gate, w_up, w_down)))
    seq_total = MICRO * SEQS_MB
    sequences = jnp.transpose(hidden_in.astype(jnp.float32), (0, 2, 1, 3)).reshape(seq_total, LENGTH, D)
    cotangents = jnp.transpose(out_grad.astype(jnp.float32), (0, 2, 1, 3)).reshape(seq_total, LENGTH, D)
    starts_all = piece_starts.reshape(seq_total, NPIECE)

    def one_sequence(totals, inputs_now):
        sequence, cotangent, starts = inputs_now

        def forward(seq_in, *weights):
            return layer(seq_in, starts, *weights)
        result, pullback = jax.vjp(forward, sequence, *params)
        grads = pullback(cotangent)
        summed = tuple((running + update for running, update in zip(totals, grads[1:])))
        return (summed, (result.astype(jnp.bfloat16), grads[0]))
    zeros_init = tuple((jnp.zeros_like(member) for member in params))
    totals, (results, in_grads) = lax.scan(one_sequence, zeros_init, (sequences, cotangents, starts_all))
    hidden_out = jnp.transpose(results.reshape(MICRO, SEQS_MB, LENGTH, D), (0, 2, 1, 3))
    in_grad = jnp.transpose(in_grads.reshape(MICRO, SEQS_MB, LENGTH, D), (0, 2, 1, 3))
    return (hidden_out, in_grad, totals[0], totals[1], totals[2], totals[3], totals[4], totals[5], totals[6], totals[7], totals[8])
```

```python
import functools
import math

import jax
import jax.numpy as jnp
from jax import lax
from jax.experimental import pallas as pl
from jax.experimental.pallas import tpu as pltpu
from jax.sharding import PartitionSpec as P

HQ = 9
KVH = 3
HD = 64
PIECE = 256


EPS = 1e-05
MASKED = -1e30


def product(left, right):
    return jnp.dot(left, right, preferred_element_type=jnp.float32)


def rope_tables(positions, head_dim):
    halfway = head_dim // 2
    frequency = 10000.0 ** (-jnp.arange(halfway, dtype=jnp.float32) / halfway)
    angles = positions.astype(jnp.float32)[:, None] * frequency[None, :]
    return (jnp.cos(angles), jnp.sin(angles))


def rotate(values, cosine, sine_tab):
    halfway = values.shape[-1] // 2
    former = values[..., :halfway]
    latter = values[..., halfway:]
    cosine = cosine[:, None, None, :]
    sine_tab = sine_tab[:, None, None, :]
    return jnp.concatenate(
        [former * cosine - latter * sine_tab, latter * cosine + former * sine_tab], axis=-1
    )


def piece_labels(positions, starts):
    inside = (positions[None, :, None] >= starts[:, None, :]) & (
        positions[None, :, None] < starts[:, None, :] + PIECE
    )
    numbers = jnp.arange(1, starts.shape[1] + 1, dtype=jnp.int32)
    return jnp.sum(jnp.where(inside, numbers[None, None, :], 0), axis=2) - 1


def group_rows(values, groups):
    local_len, seq_dp = (values.shape[0], values.shape[1])
    shaped = values.reshape(local_len, seq_dp, KVH, groups, HD)
    return shaped.transpose(1, 2, 0, 3, 4).reshape(seq_dp, KVH, local_len * groups, HD)


def ungroup_rows(values, local_len):
    seq_dp = values.shape[0]
    groups = values.shape[2] // local_len
    shaped = values.reshape(seq_dp, KVH, local_len, groups, HD)
    return shaped.transpose(2, 0, 1, 3, 4).reshape(local_len, seq_dp, KVH * groups * HD)


def split_pairs(block):
    key_rows = block[..., : KVH * HD].reshape(block.shape[0], block.shape[1], KVH, HD)
    value_rows = block[..., KVH * HD :].reshape(block.shape[0], block.shape[1], KVH, HD)
    return (key_rows, value_rows)


def block_mask(query_pos, query_labels, key_pos, key_labels):
    causal = key_pos[None, None, :] <= query_pos[None, :, None]
    shared = (query_labels[:, :, None] == key_labels[:, None, :]) & (query_labels[:, :, None] >= 0)
    return (causal | shared)[:, None]


def norm_back(grad_in, rows_in, row_scale, gain_vec):
    scaled = grad_in * gain_vec
    gain_grad = jnp.sum(grad_in * rows_in * row_scale, axis=0)
    input_grad = row_scale * scaled - rows_in * row_scale**3 * jnp.mean(
        scaled * rows_in, axis=1, keepdims=True
    )
    return (input_grad, gain_grad)


def forward_pass(block_in, starts, full_set, positions, cosine, sine_tab, query_pos):
    gain_one, w_query, w_key, w_value, w_out, gain_two, w_gate, w_up, w_down = full_set
    local_len, seq_dp, width = block_in.shape
    groups = HQ // KVH
    rows_in = block_in.astype(jnp.float32).reshape(local_len * seq_dp, width)
    scale_one = lax.rsqrt(jnp.mean(rows_in * rows_in, axis=1, keepdims=True) + EPS)
    normed = (rows_in * scale_one * gain_one.astype(jnp.float32)).astype(jnp.bfloat16)
    queries = product(normed, w_query).reshape(local_len, seq_dp, HQ, HD)
    key_pre = product(normed, w_key).reshape(local_len, seq_dp, KVH, HD)
    value_low = product(normed, w_value).astype(jnp.bfloat16)
    query_grp = group_rows(rotate(queries, cosine, sine_tab).astype(jnp.bfloat16), groups)
    key_low = (
        rotate(key_pre, cosine, sine_tab).astype(jnp.bfloat16).reshape(local_len, seq_dp, KVH * HD)
    )
    key_vals = jnp.concatenate([key_low, value_low.reshape(local_len, seq_dp, KVH * HD)], axis=2)
    query_labels = jnp.repeat(piece_labels(positions, starts), groups, axis=1)
    rows_q = local_len * groups

    def absorb(state, block, key_start):
        key_rows, value_rows = split_pairs(block)
        key_pos = key_start + jnp.arange(block.shape[0], dtype=jnp.int32)
        allowed = block_mask(query_pos, query_labels, key_pos, piece_labels(key_pos, starts))
        best, total_w, summed = state
        scores = (
            jnp.einsum("snrd,ksnd->snrk", query_grp, key_rows, preferred_element_type=jnp.float32)
            * 0.125
        )
        masked = jnp.where(allowed, scores, MASKED)
        new_best = jnp.maximum(best, jnp.max(masked, axis=3))
        expo = jnp.where(allowed, jnp.exp(masked - new_best[..., None]), 0.0)
        fade = jnp.exp(best - new_best)
        total_w = total_w * fade + jnp.sum(expo, axis=3)
        summed = summed * fade[..., None] + jnp.einsum(
            "snrk,ksnd->snrd",
            expo.astype(jnp.bfloat16),
            value_rows,
            preferred_element_type=jnp.float32,
        )
        return (new_best, total_w, summed)

    start_state = (
        jnp.full((seq_dp, KVH, rows_q), MASKED, jnp.float32),
        jnp.zeros((seq_dp, KVH, rows_q), jnp.float32),
        jnp.zeros((seq_dp, KVH, rows_q, HD), jnp.float32),
    )
    segment = lax.all_gather(key_vals, "ctx", axis=0, tiled=True)
    step_len = math.gcd(segment.shape[0], 512)

    def fold_one_block(block_no, state):
        block = lax.dynamic_slice_in_dim(segment, block_no * step_len, step_len, 0)
        return absorb(state, block, block_no * step_len)

    best, total_w, summed = lax.fori_loop(
        0, segment.shape[0] // step_len, fold_one_block, start_state
    )
    attn_grp = summed / total_w[..., None]
    log_total = best + jnp.log(total_w)
    attn_low = (
        ungroup_rows(attn_grp, local_len).reshape(local_len * seq_dp, HQ * HD).astype(jnp.bfloat16)
    )
    middle = rows_in + product(attn_low, w_out)
    scale_two = lax.rsqrt(jnp.mean(middle * middle, axis=1, keepdims=True) + EPS)
    normed_two = (middle * scale_two * gain_two.astype(jnp.float32)).astype(jnp.bfloat16)
    gate_pre = product(normed_two, w_gate)
    upward = product(normed_two, w_up)
    hidden = (gate_pre * jax.nn.sigmoid(gate_pre) * upward).astype(jnp.bfloat16)
    result = (
        (middle + product(hidden, w_down)).astype(jnp.bfloat16).reshape(local_len, seq_dp, width)
    )
    saved = (
        rows_in,
        scale_one,
        normed,
        query_grp,
        key_vals,
        attn_grp,
        attn_low,
        log_total,
        middle,
        scale_two,
        normed_two,
        gate_pre,
        upward,
        hidden,
        query_labels,
    )
    return (saved, result)


def backward_pass(cotangent, starts, full_set, saved, cosine, sine_tab, query_pos):
    gain_one, w_query, w_key, w_value, w_out, gain_two, w_gate, w_up, w_down = full_set
    (
        rows_in,
        scale_one,
        normed,
        query_grp,
        key_vals,
        attn_grp,
        attn_low,
        log_total,
        middle,
        scale_two,
        normed_two,
        gate_pre,
        upward,
        hidden,
        query_labels,
    ) = saved
    local_len, seq_dp, width = cotangent.shape
    groups = HQ // KVH
    cot_rows = cotangent.reshape(local_len * seq_dp, width)
    grad_down = product(hidden.T, cot_rows)
    grad_hidden = product(cot_rows, w_down.T)
    sigma = jax.nn.sigmoid(gate_pre)
    grad_gate = (grad_hidden * upward * sigma * (1.0 + gate_pre * (1.0 - sigma))).astype(
        jnp.bfloat16
    )
    grad_upward = (grad_hidden * gate_pre * sigma).astype(jnp.bfloat16)
    grad_wgate = product(normed_two.T, grad_gate)
    grad_wup = product(normed_two.T, grad_upward)
    grad_normed_two = product(grad_gate, w_gate.T) + product(grad_upward, w_up.T)
    mid_part, grad_gain_two = norm_back(
        grad_normed_two, middle, scale_two, gain_two.astype(jnp.float32)
    )
    grad_middle = cot_rows.astype(jnp.float32) + mid_part
    branch_low = grad_middle.astype(jnp.bfloat16)
    grad_wout = product(attn_low.T, branch_low)
    grad_attn = group_rows(
        product(branch_low, w_out.T).astype(jnp.bfloat16).reshape(local_len, seq_dp, HQ, HD), groups
    )
    delta = jnp.sum(grad_attn.astype(jnp.float32) * attn_grp, axis=3)
    key_all = lax.all_gather(key_vals, "ctx", axis=0, tiled=True)
    seq_len = key_all.shape[0]
    step_len = math.gcd(seq_len, 512)

    def backward_one_block(block_no, state):
        anchor = block_no * step_len
        block = lax.dynamic_slice_in_dim(key_all, anchor, step_len, 0)
        key_rows, value_rows = split_pairs(block)
        key_pos = anchor + jnp.arange(step_len, dtype=jnp.int32)
        allowed = block_mask(query_pos, query_labels, key_pos, piece_labels(key_pos, starts))
        grad_query, grad_pairs = state
        scores = (
            jnp.einsum("snrd,ksnd->snrk", query_grp, key_rows, preferred_element_type=jnp.float32)
            * 0.125
        )
        probs = jnp.where(allowed, jnp.exp(scores - log_total[..., None]), 0.0)
        grad_probs = jnp.einsum(
            "snrd,ksnd->snrk", grad_attn, value_rows, preferred_element_type=jnp.float32
        )
        grad_scores = (probs * (grad_probs - delta[..., None])).astype(jnp.bfloat16)
        grad_query = (
            grad_query
            + jnp.einsum(
                "snrk,ksnd->snrd", grad_scores, key_rows, preferred_element_type=jnp.float32
            )
            * 0.125
        )
        grad_keys = (
            jnp.einsum(
                "snrk,snrd->ksnd", grad_scores, query_grp, preferred_element_type=jnp.float32
            )
            * 0.125
        )
        grad_values = jnp.einsum(
            "snrk,snrd->ksnd",
            probs.astype(jnp.bfloat16),
            grad_attn,
            preferred_element_type=jnp.float32,
        )
        pair_block = jnp.concatenate(
            [
                grad_keys.reshape(step_len, seq_dp, KVH * HD),
                grad_values.reshape(step_len, seq_dp, KVH * HD),
            ],
            axis=2,
        )
        grad_pairs = lax.dynamic_update_slice_in_dim(grad_pairs, pair_block, anchor, 0)
        return (grad_query, grad_pairs)

    start_state = (
        jnp.zeros(query_grp.shape, jnp.float32),
        jnp.zeros((seq_len, seq_dp, 2 * KVH * HD), jnp.float32),
    )
    grad_query, grad_pairs = lax.fori_loop(0, seq_len // step_len, backward_one_block, start_state)
    pair_local = lax.psum_scatter(grad_pairs, "ctx", scatter_dimension=0, tiled=True)
    grad_key_rot = pair_local[..., : KVH * HD].reshape(local_len, seq_dp, KVH, HD)
    grad_value = (
        pair_local[..., KVH * HD :].reshape(local_len * seq_dp, KVH * HD).astype(jnp.bfloat16)
    )
    grad_key = (
        rotate(grad_key_rot, cosine, -sine_tab)
        .astype(jnp.bfloat16)
        .reshape(local_len * seq_dp, KVH * HD)
    )
    query_rot = ungroup_rows(grad_query, local_len).reshape(local_len, seq_dp, HQ, HD)
    grad_query_rows = (
        rotate(query_rot, cosine, -sine_tab)
        .astype(jnp.bfloat16)
        .reshape(local_len * seq_dp, HQ * HD)
    )
    grad_wquery = product(normed.T, grad_query_rows)
    grad_wkey = product(normed.T, grad_key)
    grad_wvalue = product(normed.T, grad_value)
    grad_normed = (
        product(grad_query_rows, w_query.T)
        + product(grad_key, w_key.T)
        + product(grad_value, w_value.T)
    )
    in_part, grad_gain_one = norm_back(
        grad_normed, rows_in, scale_one, gain_one.astype(jnp.float32)
    )
    grad_input = (grad_middle + in_part).reshape(local_len, seq_dp, width)
    grads = (
        grad_gain_one,
        grad_wquery,
        grad_wkey,
        grad_wvalue,
        grad_wout,
        grad_gain_two,
        grad_wgate,
        grad_wup,
        grad_down,
    )
    return (grads, grad_input)


def general_body(
    hidden_in,
    piece_starts,
    out_grad,
    attn_gain,
    w_query,
    w_key,
    w_value,
    w_out,
    mlp_gain,
    w_gate,
    w_up,
    w_down,
):
    micro_count, local_len = (hidden_in.shape[0], hidden_in.shape[1])
    groups = HQ // KVH
    positions = lax.axis_index("ctx") * local_len + jnp.arange(local_len, dtype=jnp.int32)
    cosine, sine_tab = rope_tables(positions, HD)
    query_pos = jnp.repeat(positions, groups)
    ctx_devices = lax.axis_size("ctx")
    shards = (attn_gain, w_query, w_key, w_value, w_out, mlp_gain, w_gate, w_up, w_down)
    totals = [
        jnp.zeros((member.shape[0] * ctx_devices,) + member.shape[1:], jnp.float32)
        for member in shards
    ]
    outputs_fwd = []
    outputs_back = []
    for micro_no in range(micro_count):
        fenced = lax.optimization_barrier(
            (attn_gain, w_query, w_key, w_value, w_out, mlp_gain, w_gate, w_up, w_down, totals[0])
        )
        full_set = (
            lax.all_gather(fenced[0], "ctx", axis=0, tiled=True),
            lax.all_gather(fenced[1], "ctx", axis=0, tiled=True),
            lax.all_gather(fenced[2], "ctx", axis=0, tiled=True),
            lax.all_gather(fenced[3], "ctx", axis=0, tiled=True),
            lax.all_gather(fenced[4], "ctx", axis=0, tiled=True),
            lax.all_gather(fenced[5], "ctx", axis=0, tiled=True),
            lax.all_gather(fenced[6], "ctx", axis=0, tiled=True),
            lax.all_gather(fenced[7], "ctx", axis=0, tiled=True),
            lax.all_gather(fenced[8], "ctx", axis=0, tiled=True),
        )
        saved, result = forward_pass(
            hidden_in[micro_no],
            piece_starts[micro_no],
            full_set,
            positions,
            cosine,
            sine_tab,
            query_pos,
        )
        fenced = lax.optimization_barrier(
            (attn_gain, w_query, w_key, w_value, w_out, mlp_gain, w_gate, w_up, w_down, result)
        )
        full_set = (
            lax.all_gather(fenced[0], "ctx", axis=0, tiled=True),
            lax.all_gather(fenced[1], "ctx", axis=0, tiled=True),
            lax.all_gather(fenced[2], "ctx", axis=0, tiled=True),
            lax.all_gather(fenced[3], "ctx", axis=0, tiled=True),
            lax.all_gather(fenced[4], "ctx", axis=0, tiled=True),
            lax.all_gather(fenced[5], "ctx", axis=0, tiled=True),
            lax.all_gather(fenced[6], "ctx", axis=0, tiled=True),
            lax.all_gather(fenced[7], "ctx", axis=0, tiled=True),
            lax.all_gather(fenced[8], "ctx", axis=0, tiled=True),
        )
        grads, grad_input = backward_pass(
            out_grad[micro_no], piece_starts[micro_no], full_set, saved, cosine, sine_tab, query_pos
        )
        totals = [running + update for running, update in zip(totals, grads)]
        outputs_fwd.append(result)
        outputs_back.append(grad_input)
    reduced = (
        lax.psum_scatter(totals[0], "ctx", scatter_dimension=0, tiled=True),
        lax.psum_scatter(totals[1], "ctx", scatter_dimension=0, tiled=True),
        lax.psum_scatter(totals[2], "ctx", scatter_dimension=0, tiled=True),
        lax.psum_scatter(totals[3], "ctx", scatter_dimension=0, tiled=True),
        lax.psum_scatter(totals[4], "ctx", scatter_dimension=0, tiled=True),
        lax.psum_scatter(totals[5], "ctx", scatter_dimension=0, tiled=True),
        lax.psum_scatter(totals[6], "ctx", scatter_dimension=0, tiled=True),
        lax.psum_scatter(totals[7], "ctx", scatter_dimension=0, tiled=True),
        lax.psum_scatter(totals[8], "ctx", scatter_dimension=0, tiled=True),
    )
    owned = (
        lax.psum(reduced[0].astype(jnp.bfloat16), "dp").astype(jnp.float32),
        lax.psum(reduced[1].astype(jnp.bfloat16), "dp").astype(jnp.float32),
        lax.psum(reduced[2].astype(jnp.bfloat16), "dp").astype(jnp.float32),
        lax.psum(reduced[3].astype(jnp.bfloat16), "dp").astype(jnp.float32),
        lax.psum(reduced[4].astype(jnp.bfloat16), "dp").astype(jnp.float32),
        lax.psum(reduced[5].astype(jnp.bfloat16), "dp").astype(jnp.float32),
        lax.psum(reduced[6].astype(jnp.bfloat16), "dp").astype(jnp.float32),
        lax.psum(reduced[7].astype(jnp.bfloat16), "dp").astype(jnp.float32),
        lax.psum(reduced[8].astype(jnp.bfloat16), "dp").astype(jnp.float32),
    )
    return (
        jnp.stack(outputs_fwd),
        jnp.stack(outputs_back),
        owned[0],
        owned[1],
        owned[2],
        owned[3],
        owned[4],
        owned[5],
        owned[6],
        owned[7],
        owned[8],
    )


F32 = jnp.float32
BF16 = jnp.bfloat16
NT = (((1,), (1,)), ((), ()))
IN_VMEM = pl.BlockSpec(memory_space=pltpu.VMEM)
IN_SMEM = pl.BlockSpec(memory_space=pltpu.SMEM)
IN_HBM = pl.BlockSpec(memory_space=pltpu.HBM)
ANYWHERE = pl.BlockSpec(memory_space=pl.ANY)


def nt_dot(left, right):
    return lax.dot_general(left, right, NT, preferred_element_type=F32)


def call(kernel, outs, scalars, arrays, scratch=(), limit=6, micros=0.5, name=None):
    specs, flat = [], []
    for spec, group in arrays:
        specs += [spec] * len(group)
        if spec is IN_HBM:
            group = [pltpu.with_memory_space_constraint(item, pltpu.HBM) for item in group]
        flat += group
    return pl.pallas_call(
        kernel,
        out_shape=tuple(jax.ShapeDtypeStruct(*out) for out in outs),
        in_specs=[IN_SMEM] * len(scalars) + specs,
        out_specs=tuple(IN_VMEM for _ in outs),
        scratch_shapes=list(scratch),
        name=name,
        compiler_params=pltpu.CompilerParams(vmem_limit_bytes=limit << 20),
        cost_estimate=pl.CostEstimate(
            flops=1000, bytes_accessed=int(3_600_000 * micros), transcendentals=0
        ),
    )(*scalars, *flat)


def start_all(pairs, sems, first=0):
    copies = [
        pltpu.make_async_copy(src, dst, sems.at[first + i]) for i, (src, dst) in enumerate(pairs)
    ]
    for item in copies:
        item.start()
    return copies


def wait_all(copies):
    for item in copies:
        item.wait()


def rows_of(ref):
    return jnp.concatenate([ref[m].astype(F32).T for m in range(ref.shape[0])], axis=0)


def turn(block, cosine, sine):
    half = HD // 2
    former, latter = block[:half], block[half:]
    return former * cosine - latter * sine, latter * cosine + former * sine


def pack_kernel(gate_ref, up_ref, out_ref, down_ref, wide_ref, narrow_ref, out_now, down_now, sems):
    rows, ff = gate_ref.shape
    width = out_ref.shape[1]
    wait_all(
        start_all(
            [
                (gate_ref, wide_ref.at[:, :ff]),
                (up_ref, wide_ref.at[:, ff : 2 * ff]),
                (out_ref, out_now),
                (down_ref, down_now),
            ],
            sems,
        )
    )
    narrow_ref[:, :width] = out_now[...]
    for c in range(3):
        base = (c + 1) * width
        count = min(rows, down_now.shape[0] - c * rows)
        narrow_ref[:count, base : base + width] = down_now[c * rows : c * rows + count, :]


def project_kernel(rows_w, me_ref, x_ref, *refs):
    pieces, (cos_ref, sin_ref, q_ref, kv_ref, w_ref, gain_ref) = refs[:8], refs[8:]
    me = me_ref[0]
    for r in range(8):
        w_ref[pl.ds(pl.multiple_of((me ^ r) * rows_w, 8), rows_w), :] = pieces[r][...]
    rows = rows_of(x_ref)
    gains = w_ref[:, 896:1024].astype(F32).T
    gain_ref[...] = gains[64:72]
    scale = lax.rsqrt(jnp.mean(rows * rows, axis=1, keepdims=True) + EPS)
    normed = (rows * scale * gains[64:65]).astype(BF16)
    turned = jnp.dot(normed, w_ref[...], preferred_element_type=F32).T
    cosine, sine = cos_ref[...], sin_ref[...]
    half = HD // 2
    for head in range(HQ + KVH):
        base = head * HD
        upper, lower = turn(turned[base : base + HD], cosine, sine)
        if head < HQ:
            q_ref[base : base + half, :] = (upper * 0.125).astype(BF16)
            q_ref[base + half : base + HD, :] = (lower * 0.125).astype(BF16)
        else:
            base -= HQ * HD
            kv_ref[base : base + half, :] = upper.astype(BF16)
            kv_ref[base + half : base + HD, :] = lower.astype(BF16)
    kv_ref[KVH * HD :, :] = turned[(HQ + KVH) * HD : (HQ + 2 * KVH) * HD].astype(BF16)


def stack_heads(ref, group, cols):
    return jnp.concatenate(
        [ref[h * HD : (h + 1) * HD, cols] for h in range(3 * group, 3 * group + 3)], axis=1
    )


def allowed_mask(me, bound_row):
    spot = lax.broadcasted_iota(jnp.int32, (128, 384), 0)
    bound = jnp.concatenate([bound_row] * 3, axis=1)
    return jnp.concatenate([spot <= (bound - (me ^ r) * 128) for r in range(8)], axis=0)


def attend_kernel(me_ref, bound_ref, q_ref, *refs):
    pieces, (o_ref, lse_ref, kv_ref) = refs[:8], refs[8:]
    me = me_ref[0]
    for m in range(2):
        for r in range(8):
            kv_ref[m, :, r * 128 : (r + 1) * 128] = pieces[r][:, m * 128 : (m + 1) * 128]
    for m in range(2):
        cols = slice(m * 128, (m + 1) * 128)
        mask = allowed_mask(me, bound_ref[0:1, cols])
        for g in range(KVH):
            keys = kv_ref[m, g * HD : (g + 1) * HD, :].T
            values = kv_ref[m, (KVH + g) * HD : (KVH + g + 1) * HD, :]
            scores = jnp.dot(keys, stack_heads(q_ref, g, cols), preferred_element_type=F32)
            scores = jnp.where(mask, scores, MASKED)
            best = jnp.max(scores, axis=0, keepdims=True)
            expo = jnp.exp(scores - best)
            total = jnp.sum(expo, axis=0, keepdims=True)
            mixed = jnp.dot(values, expo.astype(BF16), preferred_element_type=F32) / total
            lse = best + jnp.log(total)
            for j in range(3):
                h = 3 * g + j
                part = slice(j * 128, (j + 1) * 128)
                o_ref[h * HD : (h + 1) * HD, cols] = mixed[:, part].astype(BF16)
                lse_ref[h : h + 1, cols] = lse[:, part]


def middle_kernel(rows_w, rows_d, me_ref, x_ref, dy_ref, o_ref, gain_ref, *refs):
    wides, narrows = refs[:8], refs[8:16]
    out_ref, dh_ref, do_ref, gg_ref, a_keep, a_send, b_keep, b_send = refs[16:24]
    gu, wo, wd, turned, so = refs[24:]
    me = me_ref[0]
    ff = gu.shape[1] // 2
    width = x_ref.shape[1]

    def at_row(value):
        return pl.multiple_of(value, 8)

    for r in range(8):
        peer = me ^ r
        rows = pl.ds(at_row(peer * rows_w), rows_w)
        wo[rows, :] = narrows[r][:, :width]
        gu[rows, :] = wides[r][...]
        for c in range(3):
            base = (c + 1) * width
            count = min(rows_w, rows_d - c * rows_w)
            wd[pl.ds(at_row(peer * rows_d + c * rows_w), count), :] = narrows[r][:count, base : base + width]

    def store(r, refs, base, source, offset, count):
        dst = refs[r % 2]
        size = source.shape[1]
        dst[r // 2, :count, base : base + size] = source[pl.ds(at_row(offset), count), :]

    a_refs, b_refs = (a_keep, a_send), (b_keep, b_send)
    gain = gain_ref[1:2, :]
    attn = o_ref[...].T
    out_rel = jnp.concatenate(
        [o_ref[pl.ds(at_row((me ^ r) * rows_w), rows_w), :] for r in range(8)], axis=0
    )
    wo_now = wo[...]
    middle = rows_of(x_ref) + jnp.dot(attn, wo_now, preferred_element_type=F32)
    scale = lax.rsqrt(jnp.mean(middle * middle, axis=1, keepdims=True) + EPS)
    normed = (middle * scale * gain).astype(BF16)
    turned[...] = normed.T
    normed_t = jnp.concatenate(
        [turned[pl.ds(at_row((me ^ r) * rows_w), rows_w), :] for r in range(8)], axis=0
    )
    cot_wide = rows_of(dy_ref)
    cot = cot_wide.astype(BF16)
    result = middle
    back = jnp.zeros_like(middle)
    step = 768
    for b in range(ff // step):
        cg = slice(b * step, (b + 1) * step)
        cu = slice(ff + b * step, ff + (b + 1) * step)
        down = wd[cg, :]
        gate = jnp.dot(normed, gu[:, cg], preferred_element_type=F32)
        up = jnp.dot(normed, gu[:, cu], preferred_element_type=F32)
        sigma = 1.0 / (1.0 + jnp.exp(-gate))
        silu = gate * sigma
        hidden = (silu * up).astype(BF16)
        result = result + jnp.dot(hidden, down, preferred_element_type=F32)
        d_hidden = nt_dot(cot, down)
        d_gate = (d_hidden * up * sigma * (1.0 + gate * (1.0 - sigma))).astype(BF16)
        d_up = (d_hidden * silu).astype(BF16)
        back = back + nt_dot(d_gate, gu[:, cg]) + nt_dot(d_up, gu[:, cu])
        for cols, grad in ((cg, d_gate), (cu, d_up)):
            found = jnp.dot(normed_t, grad, preferred_element_type=F32).astype(BF16)
            for r in range(8):
                a_refs[r % 2][r // 2, :, cols] = found[r * rows_w : (r + 1) * rows_w]
        so[cg, :] = jnp.dot(hidden.T, cot, preferred_element_type=F32).astype(BF16)
    for r in range(8):
        for c in range(3):
            store(
                r,
                b_refs,
                (c + 1) * width,
                so,
                (me ^ r) * rows_d + c * rows_w,
                min(rows_w, rows_d - c * rows_w),
            )
    for m in range(out_ref.shape[0]):
        out_ref[m] = result[m * 128 : (m + 1) * 128].T.astype(BF16)
    gg_ref[...] = jnp.broadcast_to(
        jnp.sum(back * middle * scale, axis=0, keepdims=True), gg_ref.shape
    )
    scaled = back * gain
    d_middle = (
        cot_wide
        + scale * scaled
        - middle * (scale * scale * scale) * jnp.mean(scaled * middle, axis=1, keepdims=True)
    )
    dh_ref[...] = d_middle
    branch = d_middle.astype(BF16)
    do_ref[...] = nt_dot(wo_now, branch).astype(BF16)
    found = jnp.dot(out_rel, branch, preferred_element_type=F32).astype(BF16)
    for r in range(8):
        b_refs[r % 2][r // 2, :, :width] = found[r * rows_w : (r + 1) * rows_w]


def attend_back_kernel(
    m, me_ref, bound_ref, q_ref, o_ref, do_ref, lse_ref, cos_ref, sin_ref, kv_ref, *refs
):
    dq_ref, keep_ref, send_ref = refs
    me = me_ref[0]
    half = HD // 2
    cols = slice(m * 128, (m + 1) * 128)
    mask = allowed_mask(me, bound_ref[0:1, cols])
    cosine, sine = cos_ref[:, cols], sin_ref[:, cols]
    for g in range(KVH):
        keys_t = kv_ref[m, g * HD : (g + 1) * HD, :]
        values_t = kv_ref[m, (KVH + g) * HD : (KVH + g + 1) * HD, :]
        query, d_out = stack_heads(q_ref, g, cols), stack_heads(do_ref, g, cols)
        lse = jnp.concatenate([lse_ref[h : h + 1, cols] for h in range(3 * g, 3 * g + 3)], axis=1)
        delta = jnp.sum(
            d_out.astype(F32) * stack_heads(o_ref, g, cols).astype(F32), axis=0, keepdims=True
        )
        scores = jnp.dot(keys_t.T, query, preferred_element_type=F32)
        probs = jnp.where(mask, jnp.exp(scores - lse), 0.0)
        d_probs = jnp.dot(values_t.T, d_out, preferred_element_type=F32)
        d_scores = (probs * (d_probs - delta)).astype(BF16)
        d_query = jnp.dot(keys_t, d_scores, preferred_element_type=F32) * 0.125
        d_keys = nt_dot(query, d_scores)
        d_values = nt_dot(d_out, probs.astype(BF16))
        for j in range(3):
            base = (3 * g + j) * HD
            upper, lower = turn(d_query[:, j * 128 : (j + 1) * 128], cosine, -sine)
            dq_ref[base : base + half, :] = upper.astype(BF16)
            dq_ref[base + half : base + HD, :] = lower.astype(BF16)
        for r in range(8):
            dst = send_ref if r % 2 else keep_ref
            part = slice(r * 128, (r + 1) * 128)
            dst[r // 2, g * HD : (g + 1) * HD, :] = d_keys[:, part].astype(BF16)
            base = (KVH + g) * HD
            dst[r // 2, base : base + HD, :] = d_values[:, part].astype(BF16)


def project_back_kernel(
    rows_w, me_ref, x_ref, dh_ref, dq_0, dq_1, own_0, own_1, gg_ref, w_ref, gain_ref, cos_ref, sin_ref, *refs
):
    half_0, last_0, half_1, last_1, in_ref, keep_ref, send_ref, cot_t, grads = refs
    me = me_ref[0]
    half, query_rows, key_rows = HD // 2, HQ * HD, KVH * HD
    pairs = []
    for own, half_part, last in ((own_0, half_0, last_0), (own_1, half_1, last_1)):
        pairs.append(own[...] + half_part[0].astype(F32) + last[...].astype(F32))
    d_pair = jnp.concatenate(pairs, axis=1)
    for m, ref in enumerate((dq_0, dq_1)):
        cot_t[:query_rows, m * 128 : (m + 1) * 128] = ref[...]
    cosine, sine = cos_ref[...], sin_ref[...]
    for g in range(KVH):
        upper, lower = turn(d_pair[g * HD : (g + 1) * HD], cosine, -sine)
        base = query_rows + g * HD
        cot_t[base : base + half, :] = upper.astype(BF16)
        cot_t[base + half : base + HD, :] = lower.astype(BF16)
    cot_t[query_rows + key_rows : query_rows + 2 * key_rows, :] = d_pair[key_rows:].astype(BF16)
    cot_t[query_rows + 2 * key_rows :, :] = jnp.zeros((64, cot_t.shape[1]), BF16)
    rows = rows_of(x_ref)
    gain = gain_ref[0:1, :]
    scale = lax.rsqrt(jnp.mean(rows * rows, axis=1, keepdims=True) + EPS)
    unit = rows * scale
    normed_t = (unit * gain).astype(BF16).T
    cot = cot_t[...]
    back = nt_dot(cot.T, w_ref[...])
    grads[...] = nt_dot(normed_t, cot)
    gain_grad = jnp.sum(back * unit, axis=0, keepdims=True)
    width = gain_grad.shape[1]
    spot = lax.broadcasted_iota(jnp.int32, (128, width), 0)
    extra = jnp.where(spot == 64, gain_grad, jnp.where(spot == 65, gg_ref[0:1, :], 0.0)).T
    grads[:, 896:1024] += extra
    for r in range(8):
        off = pl.multiple_of((me ^ r) * rows_w, 8)
        dst = send_ref if r % 2 else keep_ref
        dst[r // 2] = grads[pl.ds(off, rows_w), :].astype(BF16)
    scaled = back * gain
    d_in = (
        dh_ref[...]
        + scale * scaled
        - rows * (scale * scale * scale) * jnp.mean(scaled * rows, axis=1, keepdims=True)
    )
    for m in range(in_ref.shape[0]):
        in_ref[m] = d_in[m * 128 : (m + 1) * 128].T


def near_kernel(split, keep, got, *refs):
    columns = keep.shape[2]
    low, high = {
        "both": (slice(0, columns // 2), slice(columns // 2, None)),
        "low": (slice(None), None),
        "high": (None, slice(None)),
    }[split]
    refs = list(refs)
    for cols, sent, later in ((low, (1, 3), 2), (high, (2, 3), 1)):
        if cols is not None:
            step, rest = refs.pop(0), refs.pop(0)
            for i, k in enumerate(sent):
                step[i] = (keep[k, :, cols].astype(F32) + got[k, :, cols].astype(F32)).astype(BF16)
            rest[...] = (keep[later, :, cols].astype(F32) + got[later, :, cols].astype(F32)).astype(
                BF16
            )
    refs[0][...] = keep[0].astype(F32) + got[0].astype(F32)


def near_pair_kernel(side_ref, keep, got, mine, other):
    cut = keep.shape[2] // 2
    even = side_ref[0] == 0
    for k in range(4):
        first = keep[k, :, :cut].astype(F32) + got[k, :, :cut].astype(F32)
        second = keep[k, :, cut:].astype(F32) + got[k, :, cut:].astype(F32)
        mine[k] = jnp.where(even, first, second).astype(BF16)
        other[k] = jnp.where(even, second, first).astype(BF16)


def pair_kernel(part, mine, got, step_x, rest_y, step_y, rest_x, own):
    for cols, sent, later, step, rest in (
        (slice(0, part), (1, 3), 2, step_x, rest_y),
        (slice(part, None), (2, 3), 1, step_y, rest_x),
    ):
        for i, k in enumerate(sent):
            step[i] = (mine[k, :, cols].astype(F32) + got[k, :, cols].astype(F32)).astype(BF16)
        rest[...] = (mine[later, :, cols].astype(F32) + got[later, :, cols].astype(F32)).astype(BF16)
    own[...] = mine[0].astype(F32) + got[0].astype(F32)


def join_kernel(own, half_x, last_y, half_y, last_x, out):
    part = half_x.shape[2]
    out[:, :part] = (own[:, :part] + half_x[0].astype(F32) + last_y[...].astype(F32)).astype(BF16)
    out[:, part:] = (own[:, part:] + half_y[0].astype(F32) + last_x[...].astype(F32)).astype(BF16)


def pass_kernel(*refs):
    count = len(refs) // 3
    for rest, half, out in zip(refs[:count], refs[count : 2 * count], refs[2 * count :]):
        out[...] = (rest[...].astype(F32) + half[1].astype(F32)).astype(BF16)


def split_kernel(side_ref, own, half_x, last_y, half_y, last_x, mine, other):
    cut = own.shape[1] // 2
    first = own[:, :cut] + half_x[0].astype(F32) + last_y[...].astype(F32)
    second = own[:, cut:] + half_y[0].astype(F32) + last_x[...].astype(F32)
    even = side_ref[0] == 0
    mine[...] = jnp.where(even, first, second)
    other[...] = jnp.where(even, second, first).astype(BF16)


def near_all_kernel(keep, got, out_0, out_1, out_2, out_3):
    for k, out in enumerate((out_0, out_1, out_2, out_3)):
        out[...] = (keep[k].astype(F32) + got[k].astype(F32)).astype(BF16)


def split_sum_kernel(side_ref, *refs):
    parts, (mine, other) = refs[:4], refs[4:]
    total = (parts[0][...].astype(F32) + parts[1][...].astype(F32)) + (
        parts[2][...].astype(F32) + parts[3][...].astype(F32)
    )
    cut = total.shape[1] // 2
    first, second = total[:, :cut], total[:, cut:]
    even = side_ref[0] == 0
    mine[...] = jnp.where(even, first, second)
    other[...] = jnp.where(even, second, first).astype(BF16)


def add_kernel(left, right, out):
    out[...] = (left[...].astype(F32) + right[...].astype(F32)).astype(BF16)


def joined(side_ref, mine, other):
    even = side_ref[0] == 0
    left = jnp.where(even, mine[...].astype(F32), other[...].astype(F32))
    right = jnp.where(even, other[...].astype(F32), mine[...].astype(F32))
    return jnp.concatenate([left, right], axis=1)


def unpack_wide_kernel(side_ref, ma, oa, mb, ob, gate_ref, up_ref, out_ref, down_ref):
    rows, ff = gate_ref.shape
    width = out_ref.shape[1]
    total = joined(side_ref, ma, oa)
    gate_ref[...] = total[:, :ff]
    up_ref[...] = total[:, ff:]
    total = joined(side_ref, mb, ob)
    out_ref[...] = total[:, :width]
    for c in range(3):
        begin = c * rows
        count = min(rows, down_ref.shape[0] - begin)
        base = (c + 1) * width
        down_ref[begin : begin + count, :] = total[:count, base : base + width]


def unpack_first_kernel(side_ref, mine, other, q_ref, k_ref, v_ref, gain_ref):
    total = joined(side_ref, mine, other)
    q_cols, k_cols = q_ref.shape[1], k_ref.shape[1]
    q_ref[...] = total[:, :q_cols]
    k_ref[...] = total[:, q_cols : q_cols + k_cols]
    v_ref[...] = total[:, q_cols + k_cols : q_cols + 2 * k_cols]
    gain_ref[...] = total[:, 896:1024].T[64:72]


ORDER = {"wide2": ["first2", "first4"], "wide4": ["first2", "first4", "first6"], "narrow2": ["wide2", "wide4"], "narrow4": ["wide2", "wide4"], "wide6": ["kv4"], "wide1": ["kv5"], "wide3": ["kv3", "kv5"], "wide5": ["kv3", "kv5"], "narrow1": ["kv3", "kv5"], "narrow3": ["kv3", "kv5"], "narrow5": ["kv3", "kv5"], "wide7": ["attend"], "narrow7": ["attend"], "a_near": ["back0"], "back1": ["a_near", "b_near"], "k_near0": ["a2", "a4"], "k_near1": ["a2", "a4"], "a_pass": ["k_near0", "k_near1"], "k_pass": ["a_pass", "b_pair"], "project_back": ["a_split", "b_pair", "b4"], "b_pass": ["w4", "w6", "a_add1"], "b_join": ["a_add2"], "b_add2": ["a_z3"], "w_add2": ["b_add2"], "w_near": ["b2"], "b_pair": ["a2"], "attend": ["narrow3"], "w1": ["a_z1"], "w6": ["w_near"], "w_split": ["a_add1"]}
MICROS = {"attend": 4.8, "middle": 13, "back0": 3.6, "back1": 3.6, "project": 0.5, "project_back": 2, "small": 1}


class Plan:
    def __init__(self):
        self.done = {}

    def tie(self, name, value):
        waits = [self.done[other] for other in ORDER.get(name, ()) if other in self.done]
        return lax.optimization_barrier((value, *waits))[0] if waits else value

    def swap(self, name, value, bit):
        pairs = [(i, i ^ bit) for i in range(8)]
        self.done[name] = lax.ppermute(self.tie(name, value), "ctx", pairs)
        return self.done[name]

    def swap_dp(self, name, value, bit):
        pairs = [(i, i ^ bit) for i in range(4)]
        self.done[name] = lax.ppermute(self.tie(name, value), "dp", pairs)
        return self.done[name]

    def run(self, name, kernel, outs, scalars, arrays, **options):
        (spec, group), *rest = arrays
        arrays = [(spec, [self.tie(name, group[0]), *group[1:]]), *rest]
        micros = MICROS.get(name, MICROS.get("small", 0.5))
        found = call(kernel, outs, scalars, arrays, micros=micros, name=name, **options)
        self.done[name] = found[0]
        return found


def fast_body(
    hidden_in,
    piece_starts,
    out_grad,
    attn_gain,
    w_query,
    w_key,
    w_value,
    w_out,
    mlp_gain,
    w_gate,
    w_up,
    w_down,
):
    micro, local, seqs, width = hidden_in.shape
    tokens = micro * local
    rows_w, rows_d = w_query.shape[0], w_down.shape[0]
    ff = w_gate.shape[1]
    q_cols, k_cols = HQ * HD, KVH * HD
    wide_a, wide_b = 2 * ff, 4 * width
    me = lax.axis_index("ctx").astype(jnp.int32)
    me_arr = me.reshape(1)
    side = (lax.axis_index("dp").astype(jnp.int32) & 1).reshape(1)
    w_query, me_arr, side = lax.optimization_barrier((w_query, me_arr, side))
    positions = me_arr[0] * local + jnp.arange(local, dtype=jnp.int32)
    cosine, sine = rope_tables(positions, HD)
    cos_t, sin_t = jnp.tile(cosine.T, (1, micro)), jnp.tile(sine.T, (1, micro))
    starts = piece_starts.reshape(micro, -1)
    inside = (positions[None, :, None] >= starts[:, None, :]) & (
        positions[None, :, None] < starts[:, None, :] + PIECE
    )
    ends = jnp.max(jnp.where(inside, starts[:, None, :] + (PIECE - 1), 0), axis=2)
    bound = jnp.maximum(ends, positions[None, :]).reshape(1, tokens)
    bound = jnp.broadcast_to(bound, (8, tokens))
    x = hidden_in.transpose(0, 2, 3, 1).reshape(micro, width, local)
    dy = out_grad.transpose(0, 2, 3, 1).reshape(micro, width, local)

    plan = Plan()
    gains = jnp.pad(jnp.stack([attn_gain, mlp_gain], axis=1), ((0, 0), (0, 62)))
    first = jnp.concatenate([w_query, w_key, w_value, gains], axis=1)
    far = [plan.swap(f"first{bit}", first, bit) for bit in (2, 4, 6)]
    wide, narrow = plan.run(
        "pack",
        pack_kernel,
        [((rows_w, wide_a), BF16), ((rows_w, wide_b), BF16)],
        [],
        [(IN_HBM, [w_gate, w_up, w_out, w_down])],
        scratch=[
            pltpu.VMEM((rows_w, width), BF16),
            pltpu.VMEM((rows_d, width), BF16),
            pltpu.SemaphoreType.DMA((4,)),
        ],
        limit=2,
    )
    wide_x, wide_y = plan.swap("wide2", wide, 2), plan.swap("wide4", wide, 4)
    near = [plan.swap(f"first{2 * i + 1}", part, 1) for i, part in enumerate([first] + far)]
    first_parts = [part for pair in zip([first] + far, near) for part in pair]
    q_t, kv_t, w_first, gain_rows = plan.run(
        "project",
        functools.partial(project_kernel, rows_w),
        [
            ((q_cols, tokens), BF16),
            ((2 * k_cols, tokens), BF16),
            ((width, 1024), BF16),
            ((8, width), F32),
        ],
        [me_arr],
        [(IN_VMEM, [x, *first_parts, cos_t, sin_t])],
        limit=4,
    )
    kv_x, kv_y = plan.swap("kv2", kv_t, 2), plan.swap("kv4", kv_t, 4)
    narrow_x, narrow_y = plan.swap("narrow2", narrow, 2), plan.swap("narrow4", narrow, 4)
    kv_xy = plan.swap("kv6", kv_y, 2)
    wide_xy, narrow_xy = plan.swap("wide6", wide_x, 4), plan.swap("narrow6", narrow_y, 2)
    kv_parts = []
    for i, part in enumerate((kv_t, kv_x, kv_y, kv_xy)):
        kv_parts += [part, plan.swap(f"kv{2 * i + 1}", part, 1)]
    weights = []
    for label, parts in (
        ("wide", (wide, wide_x, wide_y)),
        ("narrow", (narrow, narrow_x, narrow_y)),
    ):
        weights.append([])
        for i, part in enumerate(parts):
            weights[-1] += [part, plan.swap(f"{label}{2 * i + 1}", part, 1)]
    o_t, lse, kv_all = plan.run(
        "attend",
        attend_kernel,
        [
            ((q_cols, tokens), BF16),
            ((16, tokens), F32),
            ((micro, 2 * k_cols, 1024), BF16),
        ],
        [me_arr],
        [(IN_VMEM, [bound, q_t, *kv_parts])],
        limit=4,
    )
    weights[0] += [wide_xy, plan.swap("wide7", wide_xy, 1)]
    weights[1] += [narrow_xy, plan.swap("narrow7", narrow_xy, 1)]
    result, dh, do_t, gg, keep_a, send_a, keep_b, send_b = plan.run(
        "middle",
        functools.partial(middle_kernel, rows_w, rows_d),
        [
            ((micro, width, local), BF16),
            ((tokens, width), F32),
            ((q_cols, tokens), BF16),
            ((8, width), F32),
            ((4, rows_w, wide_a), BF16),
            ((4, rows_w, wide_a), BF16),
            ((4, rows_w, wide_b), BF16),
            ((4, rows_w, wide_b), BF16),
        ],
        [me_arr],
        [
            (IN_VMEM, [x, dy, o_t, gain_rows, *weights[0], *weights[1]]),
        ],
        scratch=[
            pltpu.VMEM((width, 2 * ff), BF16),
            pltpu.VMEM((q_cols, width), BF16),
            pltpu.VMEM((ff, width), BF16),
            pltpu.VMEM((width, tokens), BF16),
            pltpu.VMEM((ff, width), BF16),
        ],
        limit=25,
    )

    def near_sums(name, keep, got, split):
        _, rows, columns = keep.shape
        part = columns // 2 if split == "both" else columns
        shapes = [((2, rows, part), BF16), ((rows, part), BF16)] * (2 if split == "both" else 1)
        return plan.run(
            name,
            functools.partial(near_kernel, split),
            shapes + [((rows, columns), F32)],
            [],
            [(IN_VMEM, [keep, got])],
            limit=3,
        )

    def passing(name, *pairs):
        rests, halves = zip(*pairs)
        shapes = [(rest.shape, BF16) for rest in rests]
        return plan.run(name, pass_kernel, shapes, [], [(IN_VMEM, [*rests, *halves])], limit=2)

    def attend_back(m):
        return plan.run(
            f"back{m}",
            functools.partial(attend_back_kernel, m),
            [
                ((q_cols, local), BF16),
                ((4, 2 * k_cols, local), BF16),
                ((4, 2 * k_cols, local), BF16),
            ],
            [me_arr],
            [(IN_VMEM, [bound, q_t, o_t, do_t, lse, cos_t, sin_t, kv_all])],
            limit=5,
        )

    def add_pair(name, left, right):
        size = [(left.shape, BF16)]
        return plan.run(name, add_kernel, size, [], [(IN_VMEM, [left, right])], limit=2)[0]

    got_a, got_b = plan.swap("a1", send_a, 1), plan.swap("b1", send_b, 1)
    dq_0, keep_0, send_0 = attend_back(0)
    ax, apy, ay, apx, a_own = near_sums("a_near", keep_a, got_a, "both")
    ahx, ahy = plan.swap("a2", ax, 2), plan.swap("a4", ay, 4)
    pieces = (4, rows_w, wide_b // 2)
    b_mine, b_other = plan.run(
        "b_near", near_pair_kernel, [(pieces, BF16)] * 2, [side], [(IN_VMEM, [keep_b, got_b])], limit=2
    )
    b_got = plan.swap_dp("b_z", b_other, 1)
    part = wide_b // 4 // 128 * 128
    shapes = [(2, rows_w, part), (rows_w, part)]
    shapes += [(2, rows_w, wide_b // 2 - part), (rows_w, wide_b // 2 - part)]
    bx, bpy, by, bpx, b_own = plan.run(
        "b_pair",
        functools.partial(pair_kernel, part),
        [(shape, BF16) for shape in shapes] + [((rows_w, wide_b // 2), F32)],
        [],
        [(IN_VMEM, [b_mine, b_got])],
        limit=2,
    )
    bhx, bhy = plan.swap("b2", bx, 2), plan.swap("b4", by, 4)
    got_0 = plan.swap("k1_0", send_0, 1)
    dq_1, keep_1, send_1 = attend_back(1)
    got_1 = plan.swap("k1_1", send_1, 1)
    kx, kpy, k_own_0 = near_sums("k_near0", keep_0, got_0, "low")
    ky, kpx, k_own_1 = near_sums("k_near1", keep_1, got_1, "high")
    khx, khy = plan.swap("k2", kx, 2), plan.swap("k4", ky, 4)
    a_out_y, a_out_x = passing("a_pass", (apy, ahx), (apx, ahy))
    aly, alx = plan.swap("a6y", a_out_y, 4), plan.swap("a6x", a_out_x, 2)
    k_out_y, k_out_x = passing("k_pass", (kpy, khx), (kpx, khy))
    kly, klx = plan.swap("k6y", k_out_y, 4), plan.swap("k6x", k_out_x, 2)
    a_mine, a_other = plan.run(
        "a_split",
        split_kernel,
        [(alx.shape, F32), (alx.shape, BF16)],
        [side],
        [(IN_VMEM, [a_own, ahx, aly, ahy, alx])],
        limit=2,
    )
    a_half = plan.swap_dp("a_z1", a_other, 1)
    in_grad, w_keep, w_send = plan.run(
        "project_back",
        functools.partial(project_back_kernel, rows_w),
        [
            ((micro, width, local), F32),
            ((4, rows_w, 1024), BF16),
            ((4, rows_w, 1024), BF16),
        ],
        [me_arr],
        [
            (
                IN_VMEM,
                [
                    x, dh, dq_0, dq_1, k_own_0, k_own_1, gg, w_first, gain_rows,
                    cos_t, sin_t, khx, kly, khy, klx,
                ],
            ),
        ],
        scratch=[pltpu.VMEM((1024, tokens), BF16), pltpu.VMEM((width, 1024), F32)],
        limit=9,
    )
    w_got = plan.swap("w1", w_send, 1)
    size = ((rows_w, 1024), BF16)
    w_sums = plan.run(
        "w_near", near_all_kernel, [size] * 4, [], [(IN_VMEM, [w_keep, w_got])], limit=2
    )
    w_last = [w_sums[0]] + [plan.swap(f"w{2 * k}", w_sums[k], 2 * k) for k in (1, 2, 3)]
    a_pair = add_pair("a_add1", a_mine, a_half)
    a_across = plan.swap_dp("a_z2", a_pair, 2)
    a_total = add_pair("a_add2", a_pair, a_across)
    a_rest = plan.swap_dp("a_z3", a_total, 1)
    b_out_y, b_out_x = passing("b_pass", (bpy, bhx), (bpx, bhy))
    bly, blx = plan.swap("b6y", b_out_y, 4), plan.swap("b6x", b_out_x, 2)
    (b_half,) = plan.run(
        "b_join",
        join_kernel,
        [((rows_w, wide_b // 2), BF16)],
        [],
        [(IN_VMEM, [b_own, bhx, bly, bhy, blx])],
        limit=2,
    )
    b_across = plan.swap_dp("b_z2", b_half, 2)
    size = (rows_w, 512)
    w_mine, w_other = plan.run(
        "w_split", split_sum_kernel, [(size, F32), (size, BF16)], [side], [(IN_VMEM, w_last)], limit=2
    )
    w_half = plan.swap_dp("w_z1", w_other, 1)
    w_pair = add_pair("w_add1", w_mine, w_half)
    w_across = plan.swap_dp("w_z2", w_pair, 2)
    b_total = add_pair("b_add2", b_half, b_across)
    b_rest = plan.swap_dp("b_z3", b_total, 1)
    w_total = add_pair("w_add2", w_pair, w_across)
    w_rest = plan.swap_dp("w_z3", w_total, 1)
    g_gate, g_up, g_out, g_down = plan.run(
        "wide_out",
        unpack_wide_kernel,
        [((rows_w, ff), F32), ((rows_w, ff), F32), ((rows_w, width), F32), ((rows_d, width), F32)],
        [side],
        [(IN_VMEM, [a_total, a_rest, b_total, b_rest])],
        limit=4,
    )
    g_query, g_key, g_value, g_gain = plan.run(
        "first_out",
        unpack_first_kernel,
        [((rows_w, q_cols), F32), ((rows_w, k_cols), F32), ((rows_w, k_cols), F32), ((8, rows_w), F32)],
        [side],
        [(IN_VMEM, [w_total, w_rest])],
        limit=2,
    )

    def placed(value):
        return value.reshape(micro, seqs, width, local).transpose(0, 3, 1, 2)

    return (
        placed(result),
        placed(in_grad),
        g_gain[0],
        g_query,
        g_key,
        g_value,
        g_out,
        g_gain[1],
        g_gate,
        g_up,
        g_down,
    )


def body(hidden_in, piece_starts, *rest):
    fits = (
        lax.axis_size("ctx") == 8
        and lax.axis_size("dp") == 4
        and hidden_in.shape == (2, 128, 1, 576)
        and rest[8].shape == (72, 1536)
    )
    chosen = fast_body if fits else general_body
    return chosen(hidden_in, piece_starts, *rest)


def solution(mesh):
    in_specs = (
        P(None, "ctx", "dp", None),
        P(None, "dp", None),
        P(None, "ctx", "dp", None),
        P("ctx"),
        P("ctx", None),
        P("ctx", None),
        P("ctx", None),
        P("ctx", None),
        P("ctx"),
        P("ctx", None),
        P("ctx", None),
        P("ctx", None),
    )
    out_specs = (
        P(None, "ctx", "dp", None),
        P(None, "ctx", "dp", None),
        P("ctx"),
        P("ctx", None),
        P("ctx", None),
        P("ctx", None),
        P("ctx", None),
        P("ctx"),
        P("ctx", None),
        P("ctx", None),
        P("ctx", None),
    )
    return jax.shard_map(body, mesh=mesh, in_specs=in_specs, out_specs=out_specs, check_vma=False)
```
